32 devices in a mesh: dp: 8 (over z, core), resp: 4 (over y, x).
Axes of the slice: x: 2, y: 2, z: 4, core: 2. Of those that a mesh axis runs over, the one named last changes fastest.
Arguments:
- queries: bfloat16 [8, 4, 128, 4096], P('dp', 'resp'), may hold values from -6 to 6
- prefix_kv: bfloat16 [8, 256, 1024], P('dp', 'resp'), may hold values from -6 to 6
- resp_kv: bfloat16 [8, 4, 128, 1024], P('dp', 'resp'), may hold values from -6 to 6
- direction: bfloat16 [8, 4, 128, 4096], P('dp', 'resp'), may hold values from -0.09375 to 0.09375
- base_logprob: float32 [8, 4, 128], P('dp', 'resp'), may hold values from -2 to 2
- rollout_logprob: float32 [8, 4, 128], P('dp', 'resp'), may hold values from -2 to 2
- destination: int32 [8, 4, 128], P('dp', 'resp'), may hold values from 0 to 1023, as said below
- advantage: float32 [8, 4], P('dp', 'resp'), may hold values from -4 to 4
- lengths: int32 [8, 4], P('dp', 'resp'), may hold values from 1 to 128, 384 in all within a row
- prefix_blocks: int32 [8, 4], P('dp', 'resp'), may hold values from 1 to 2, as said below
Outputs:
- query_grad: bfloat16 [8, 4, 128, 4096], P('dp', 'resp')
- resp_grad: bfloat16 [8, 4, 128, 1024], P('dp', 'resp')
- prefix_grad: bfloat16 [8, 256, 1024], P('dp', 'resp')
The draws below stay inside these ranges and needn't reach their ends.
Inputs may be any that keep to these rules, and one draw needn't show every extreme that they name: For each response index r, destination maps the 1024 rollout rows one to one onto the trainer rows; value g * 128 + t names token t of prompt group g; every index of dp holds exactly 16 rows bound for each prompt group. Each response sees the leading prefix_blocks blocks of 128 prompt rows; in every prompt group some response sees all 2. In every prompt group the lengths sum to 384 and one response has 128.
All inputs are finite; a program needn't handle non-finite values.
Results may differ from the reference program's by a relative error of at most 0.011.
Values may be sent and summed in bfloat16 or wider, within the bound.
A program may use at most 128 MiB of HBM per device.

```python
import math
import jax
import jax.numpy as jnp
import numpy as np
from jax import lax

QH = 32
KVH = 4
HD = 128
GQ = 8
BLOCK = 128
R = 128
P_SIZE = 256
PB = 2
GROUPS = 8
RESPS = 4


def draw_queries(key, part):
    shape = (GROUPS, RESPS, R, KVH, GQ, HD)
    values = jnp.clip(jax.random.normal(jax.random.fold_in(key, 1), shape, jnp.float32), -6.0, 6.0)
    return values.reshape(GROUPS, RESPS, R, QH * HD).astype(jnp.bfloat16)


def draw_prefix_kv(key, part):
    shape = (GROUPS, P_SIZE, 2, KVH, HD)
    values = jnp.clip(jax.random.normal(jax.random.fold_in(key, 2), shape, jnp.float32), -6.0, 6.0)
    return values.reshape(GROUPS, P_SIZE, 2 * KVH * HD).astype(jnp.bfloat16)


def draw_destination(key, part):
    per_peer = R // GROUPS
    target_keys = jax.random.split(jax.random.fold_in(key, 3), RESPS * GROUPS)
    target_perm = jax.vmap(lambda single: jax.random.permutation(single, R))(target_keys).astype(jnp.int32)
    target_perm = target_perm.reshape(RESPS, GROUPS, GROUPS, per_peer)
    offsets = (jnp.arange(GROUPS, dtype=jnp.int32) * R)[None, :, None, None]
    by_source = (target_perm + offsets).transpose(0, 2, 1, 3).reshape(RESPS, GROUPS, R)
    source_keys = jax.random.split(jax.random.fold_in(key, 4), RESPS * GROUPS)
    source_perm = jax.vmap(lambda single: jax.random.permutation(single, R))(source_keys).astype(jnp.int32)
    shuffled = jnp.take_along_axis(by_source, source_perm.reshape(RESPS, GROUPS, R), axis=2)
    return shuffled.transpose(1, 0, 2).astype(jnp.int32)


def draw_prefix_blocks(key, part):
    counts = jax.random.randint(jax.random.fold_in(key, 17), (GROUPS, RESPS), 1, PB + 1)
    full_view = jax.random.randint(jax.random.fold_in(key, 23), (GROUPS, 1), 0, RESPS)
    return jnp.where(jnp.arange(RESPS)[None, :] == full_view, PB, counts).astype(jnp.int32)


def levels(key, dims, pieces, low, high):
    def one(position, shards_of):
        heights = jax.random.uniform(jax.random.fold_in(jax.random.fold_in(key, 6), position), (shards_of,), jnp.float32, low / len(pieces), high / len(pieces))
        return jnp.repeat(jnp.exp(heights), dims[position] // shards_of).reshape((-1,) + (1,) * (len(dims) - position - 1))

    gain = one(*pieces[0])
    for cut in pieces[1:]:
        gain = gain * one(*cut)
    return gain


def split_up(number_of, total, most, slope):
    weights = [(1 << 20) // math.isqrt(grade ** slope) + 1 for grade in range(2, number_of + 1)]
    rest, given = total - most - (number_of - 1), [1] * (number_of - 1)
    while rest > 0:
        free = [i for i in range(number_of - 1) if given[i] < most]
        pool, left = sum([weights[i] for i in free]), rest
        for i in free:
            addition = min(most - given[i], max(1, left * weights[i] // pool), rest)
            given[i] = given[i] + addition
            rest = rest - addition
    return np.array([most] + given)


def uneven_parts(rng, amount, total, most, slope):
    if amount == 2:
        one = jax.random.randint(rng, (), max(1, total - most), min(most, total - 1) + 1)
        return jnp.stack([one, total - one])
    sizes = jnp.asarray(split_up(amount, total, most, slope), jnp.int32)
    couples = (amount - 1) // 2
    donor, taker = sizes[1:1 + 2 * couples:2], sizes[2:2 + 2 * couples:2]
    room = jnp.minimum(donor - 1, most - taker)
    passed = jax.random.randint(jax.random.fold_in(rng, 1), (couples,), 0, 1 << 20) % (room + 1)
    sizes = sizes.at[1:1 + 2 * couples:2].set(donor - passed).at[2:2 + 2 * couples:2].set(taker + passed)
    return sizes[jax.random.permutation(jax.random.fold_in(rng, 2), amount)]


def noise(own_key, shape, width, most, cuts=(), kind=jnp.bfloat16):
    factor_of = levels(own_key, shape, cuts, -0.22, 0.18) if cuts else 1.0
    entries = jax.random.normal(own_key, shape, jnp.float32) * width * factor_of
    return jnp.minimum(jnp.maximum(entries, -most), most).astype(kind)


def setup_inputs(seed: int = 0) -> dict:
    key_list = jax.random.split(jax.random.key(seed), 11)
    return {
        "queries": draw_queries(jax.random.fold_in(key_list[10], 71), 0),
        "prefix_kv": draw_prefix_kv(jax.random.fold_in(key_list[10], 71), 0),
        "resp_kv": noise(key_list[2], (GROUPS, RESPS, R, 2 * KVH * HD), 1.0, 6.0, ((0, 8), (1, 4))),
        "direction": noise(key_list[3], (GROUPS, RESPS, R, QH * HD), (QH * HD) ** -0.5, 0.09375, ((0, 8), (1, 4))),
        "base_logprob": noise(key_list[4], (GROUPS, RESPS, R), 0.25, 2.0, ((0, 8), (1, 4)), jnp.float32),
        "rollout_logprob": noise(key_list[5], (GROUPS, RESPS, R), 0.25, 2.0, ((0, 8), (1, 4)), jnp.float32),
        "destination": draw_destination(jax.random.fold_in(key_list[10], 71), 0),
        "advantage": noise(key_list[7], (GROUPS, RESPS), 1.0, 4.0, ((0, 8), (1, 4)), jnp.float32),
        "lengths": jax.vmap(lambda own: uneven_parts(own, RESPS, RESPS * R * 3 // 4, R, 1))(jax.random.split(key_list[8], GROUPS)).reshape((GROUPS, RESPS)).astype(jnp.int32),
        "prefix_blocks": draw_prefix_blocks(jax.random.fold_in(key_list[10], 71), 0),
    }


loss_scale = 65536.0
clip_lower = 0.8
clip_upper = 1.28

def one_response(queries_one, keys_values, direction_rows, base_rows, old_rows, advantage_one, length_one, blocks_one):
    tok_rows = queries_one.shape[0]
    total_keys = keys_values.shape[0]
    prefix_rows = total_keys - tok_rows
    score_scale = 1.0 / math.sqrt(HD)
    key_heads = keys_values[:, :KVH * HD].reshape(total_keys, KVH, HD).astype(jnp.float32)
    value_heads = keys_values[:, KVH * HD:].reshape(total_keys, KVH, HD).astype(jnp.float32)
    query_heads = queries_one.reshape(tok_rows, KVH, GQ, HD).astype(jnp.float32)
    key_index = jnp.arange(total_keys, dtype=jnp.int32)
    query_index = jnp.arange(tok_rows, dtype=jnp.int32)
    in_prefix = (key_index < prefix_rows) & (key_index // BLOCK < blocks_one)
    in_response = (key_index[None, :] >= prefix_rows) & (key_index[None, :] - prefix_rows <= query_index[:, None])
    allowed = in_prefix[None, :] | in_response
    scores = jnp.einsum('rhgd,lhd->hgrl', query_heads, key_heads) * score_scale
    scores = jnp.where(allowed[None, None], scores, -1e+30)
    shifted = jnp.exp(scores - lax.optimization_barrier(jnp.max(scores, axis=-1, keepdims=True)))
    prob_bf16 = (shifted / lax.optimization_barrier(jnp.sum(shifted, axis=-1, keepdims=True))).astype(jnp.bfloat16)
    prob_wide = lax.optimization_barrier(prob_bf16).astype(jnp.float32)
    attn_out = jnp.einsum('hgrl,lhd->rhgd', prob_wide, value_heads)
    out_bf16 = attn_out.reshape(tok_rows, QH * HD).astype(jnp.bfloat16)
    out_wide = lax.optimization_barrier(out_bf16).astype(jnp.float32)
    new_logprob = base_rows + lax.optimization_barrier(jnp.sum(out_wide * direction_rows.astype(jnp.float32), axis=-1))
    ratio_weight = jnp.clip(jnp.exp(new_logprob - old_rows), clip_lower, clip_upper)
    loss_coeff = jnp.where(query_index < length_one, -loss_scale * ratio_weight * advantage_one / length_one.astype(jnp.float32), 0.0)
    grad_out = (loss_coeff[:, None] * direction_rows.astype(jnp.float32)).astype(jnp.bfloat16)
    grad_heads = lax.optimization_barrier(grad_out).astype(jnp.float32).reshape(tok_rows, KVH, GQ, HD)
    prob_grad = jnp.einsum('rhgd,lhd->hgrl', grad_heads, value_heads)
    row_delta = lax.optimization_barrier(jnp.sum(grad_heads * attn_out, axis=-1)).transpose(1, 2, 0)
    dscore = (prob_wide * (prob_grad - row_delta[..., None]) * score_scale).astype(jnp.bfloat16)
    dscore_wide = lax.optimization_barrier(dscore).astype(jnp.float32)
    query_grad = jnp.einsum('hgrl,lhd->rhgd', dscore_wide, key_heads).reshape(tok_rows, QH * HD).astype(jnp.bfloat16)
    key_grad = jnp.einsum('hgrl,rhgd->lhd', dscore_wide, query_heads).reshape(total_keys, KVH * HD)
    value_grad = jnp.einsum('hgrl,rhgd->lhd', prob_wide, grad_heads).reshape(total_keys, KVH * HD)
    kv_grad = jnp.concatenate([key_grad, value_grad], axis=1)
    return (query_grad, kv_grad[prefix_rows:].astype(jnp.bfloat16), kv_grad[:prefix_rows])

def place_column(where_to, values):
    return jnp.zeros((GROUPS * R,), jnp.float32).at[where_to].set(values)

def reference(queries, prefix_kv, resp_kv, direction, base_logprob, rollout_logprob, destination, advantage, lengths, prefix_blocks):
    flat_dest = destination.transpose(1, 0, 2).reshape(RESPS, GROUPS * R)
    flat_old = rollout_logprob.transpose(1, 0, 2).reshape(RESPS, GROUPS * R)
    placed = jax.vmap(place_column)(flat_dest, flat_old)
    old_logprob = placed.reshape(RESPS, GROUPS, R).transpose(1, 0, 2)

    def per_group(group_inputs):
        query_group, prefix_group, resp_group, dir_group, base_group, old_group, adv_group, len_group, block_group = group_inputs

        def per_response(running_sum, response_inputs):
            query_one, resp_one, dir_one, base_one, old_one, adv_one, len_one, block_one = response_inputs
            keys_values = jnp.concatenate([prefix_group, resp_one], axis=0)
            query_grad, resp_grad, prefix_term = one_response(query_one, keys_values, dir_one, base_one, old_one, adv_one, len_one, block_one)
            return (running_sum + prefix_term, (query_grad, resp_grad))
        prefix_total, (query_grads, resp_grads) = lax.scan(per_response, jnp.zeros((P_SIZE, 2 * KVH * HD), jnp.float32), (query_group, resp_group, dir_group, base_group, old_group, adv_group, len_group, block_group))
        return (query_grads, resp_grads, prefix_total.astype(jnp.bfloat16))
    query_grad, resp_grad, prefix_grad = lax.map(per_group, (queries, prefix_kv, resp_kv, direction, base_logprob, old_logprob, advantage, lengths, prefix_blocks))
    return (query_grad, resp_grad, prefix_grad)
```

```python
import functools
import math

import jax
import jax.numpy as jnp
from jax import lax
from jax.experimental import pallas as pl
from jax.experimental.pallas import tpu as pltpu
from jax.sharding import PartitionSpec as P

QH = 32
KVH = 4
HD = 128
GQ = 8
BLOCK = 128
PAIR = 4

loss_scale = 65536.0
clip_lower = 0.8
clip_upper = 1.28
score_scale = 1.0 / math.sqrt(HD)
exp2_scale = score_scale * math.log2(math.e)
masked = -1e30

MESH = pl.DeviceIdType.MESH
bf16, f32 = jnp.bfloat16, jnp.float32


def dot(a, b, dims):
    return lax.dot_general(a, b, (dims, ((), ())), preferred_element_type=f32)


def kernel(
    n_dp,
    n_resp,
    queries_hbm,
    prefix_hbm,
    resp_hbm,
    direction_hbm,
    base_hbm,
    rollout_hbm,
    destination_hbm,
    advantage_hbm,
    lengths_hbm,
    blocks_hbm,
    qg_ref,
    rg_ref,
    pg_ref,
    q_ref,
    d_ref,
    own_kv,
    far_kv,
    own_prob,
    far_prob,
    far_core,
    own_bias,
    far_bias,
    stats,
    rows_ref,
    own_part,
    row_send,
    row_recv,
    part_send,
    part_recv,
    base_ref,
    rollout_ref,
    destination_ref,
    advantage_ref,
    lengths_ref,
    blocks_ref,
    load_sems,
    own_sems,
    small_sems,
    prefix_send_sems,
    prefix_recv_sems,
    row_send_sems,
    row_recv_sems,
    part_send_sems,
    part_recv_sems,
    ready_sem,
):
    my_dp, my_resp = lax.axis_index("dp"), lax.axis_index("resp")
    tok = q_ref.shape[0]
    shard = prefix_hbm.shape[0]
    own_rows = own_kv.shape[0]
    far_rows = far_kv.shape[0]
    width = GQ * HD

    def head_cols(h):
        return pl.ds(h * width, width)

    def kv_cols(h, x):
        return pl.ds((x * KVH + h) * HD, HD)

    def load_copies(h):
        return (
            pltpu.make_async_copy(
                queries_hbm.at[:, head_cols(h)], q_ref.at[:, head_cols(h)], load_sems.at[h, 0]
            ),
            pltpu.make_async_copy(
                direction_hbm.at[:, head_cols(h)], d_ref.at[:, head_cols(h)], load_sems.at[h, 1]
            ),
        )

    own_copies = (
        pltpu.make_async_copy(prefix_hbm, own_kv.at[pl.ds(0, shard), :], own_sems.at[0]),
        pltpu.make_async_copy(resp_hbm, own_kv.at[pl.ds(shard, tok), :], own_sems.at[1]),
    )
    small_copies = [
        pltpu.make_async_copy(source, target, small_sems.at[i])
        for i, (source, target) in enumerate(
            (
                (blocks_hbm, blocks_ref),
                (rollout_hbm, rollout_ref),
                (destination_hbm, destination_ref),
                (base_hbm, base_ref),
                (advantage_hbm, advantage_ref),
                (lengths_hbm, lengths_ref),
            )
        )
    ]

    def resp_peer(k):
        return (my_dp, lax.rem(my_resp + k, n_resp))

    def dp_peer(k):
        return (lax.rem(my_dp + k, n_dp), my_resp)

    def prefix_copy(k, h, x):
        return pltpu.make_async_remote_copy(
            src_ref=prefix_hbm.at[:, kv_cols(h, x)],
            dst_ref=far_kv.at[pl.ds((k - 1) * shard, shard), kv_cols(h, x)],
            send_sem=prefix_send_sems.at[k - 1, h, x],
            recv_sem=prefix_recv_sems.at[k - 1, h, x],
            device_id=resp_peer(k),
            device_id_type=MESH,
        )

    def row_copy(k):
        return pltpu.make_async_remote_copy(
            src_ref=row_send,
            dst_ref=row_recv.at[k - 1],
            send_sem=row_send_sems.at[k - 1],
            recv_sem=row_recv_sems.at[k - 1],
            device_id=dp_peer(k),
            device_id_type=MESH,
        )

    def part_copy(k, h):
        return pltpu.make_async_remote_copy(
            src_ref=part_send.at[h, k - 1],
            dst_ref=part_recv.at[h, k - 1],
            send_sem=part_send_sems.at[k - 1, h],
            recv_sem=part_recv_sems.at[k - 1, h],
            device_id=resp_peer(n_resp - k),
            device_id_type=MESH,
        )

    barrier = pltpu.get_barrier_semaphore()
    for k in range(1, n_resp):
        pl.semaphore_signal(barrier, inc=1, device_id=resp_peer(k), device_id_type=MESH)
    for k in range(1, n_dp):

        @pl.when(my_dp + k < n_dp)
        def _(k=k):
            pl.semaphore_signal(barrier, inc=1, device_id=dp_peer(k), device_id_type=MESH)

    for copy in own_copies:
        copy.start()
    for h in range(KVH):
        for copy in load_copies(h):
            copy.start()
    for copy in small_copies:
        copy.start()

    pl.semaphore_wait(barrier, n_resp - 1 + my_dp)
    for h in range(KVH):
        for k in range(1, n_resp):
            for x in range(2):
                prefix_copy(k, h, x).start()
    for copy in small_copies:
        copy.wait()
    row_send[...] = jnp.zeros_like(row_send)
    row_send[0:1, :] = rollout_ref[...]
    row_send[1:2, :] = destination_ref[...].astype(f32)
    for k in range(1, n_dp):

        @pl.when(my_dp + k >= n_dp)
        def _(k=k):
            pl.semaphore_signal(ready_sem, inc=1, device_id=dp_peer(k), device_id_type=MESH)
            row_copy(k).start()

    visible = jnp.broadcast_to(blocks_ref[...], (8, tok)) * BLOCK
    visible = jnp.concatenate([visible] * (max(own_rows, far_rows) // 8), axis=0)
    key_index = lax.broadcasted_iota(jnp.int32, (own_rows, tok), 0)
    query_index = lax.broadcasted_iota(jnp.int32, (own_rows, tok), 1)
    allowed = ((key_index < shard) & (key_index + my_resp * shard < visible[:own_rows])) | (
        (key_index >= shard) & (key_index - shard <= query_index)
    )
    own_bias[...] = jnp.where(allowed, 0.0, masked)
    place = lax.broadcasted_iota(jnp.int32, (shard, tok), 0)
    for k in range(1, n_resp):
        row = place + lax.rem(my_resp + n_resp - k, n_resp) * shard
        far_bias[pl.ds((k - 1) * shard, shard), :] = jnp.where(row < visible[:shard], 0.0, masked)

    def stack(ref, h, g):
        return jnp.concatenate(
            [ref[:, pl.ds(h * width + (g + i) * HD, HD)] for i in range(PAIR)], axis=0
        )

    def scores_of(kv, bias_ref, h, g):
        bias = jnp.concatenate([bias_ref[...]] * PAIR, axis=1)
        return dot(kv[:, kv_cols(h, 0)], stack(q_ref, h, g), ((1,), (1,))) * exp2_scale + bias

    def toward_of(kv, h, g):
        return dot(kv[:, kv_cols(h, 1)], stack(d_ref, h, g), ((1,), (1,)))

    for copy in own_copies:
        copy.wait()

    for h in range(KVH):
        for copy in load_copies(h):
            copy.wait()
        for g in range(0, GQ, PAIR):
            cols = pl.ds(g * HD, PAIR * HD)
            scores = scores_of(own_kv, own_bias, h, g)
            top = jnp.max(scores, axis=0, keepdims=True)
            prob = jnp.exp2(scores - top)
            toward = toward_of(own_kv, h, g)
            stats[h, 0:1, cols] = top
            stats[h, 1:2, cols] = jnp.sum(prob, axis=0, keepdims=True)
            stats[h, 2:3, cols] = jnp.sum(prob * toward, axis=0, keepdims=True)
            own_prob[h, :, cols] = prob.astype(bf16)

    @pl.when(my_dp < n_dp - 1)
    def _():
        pl.semaphore_wait(ready_sem, n_dp - 1 - my_dp)

    for k in range(1, n_dp):

        @pl.when(my_dp + k < n_dp)
        def _(k=k):
            row_copy(k).start()

    gained = jnp.zeros((1, tok), f32)
    for h in range(KVH):
        if h == KVH - 1:
            slot = (lax.broadcasted_iota(jnp.int32, (tok, tok), 0) + my_dp * tok).astype(f32)
            placed = jnp.where(row_send[1:2, :] == slot, row_send[0:1, :], 0.0)
            for k in range(1, n_dp):
                row_copy(k).wait_recv()
                placed = placed + jnp.where(
                    row_recv[k - 1, 1:2, :] == slot, row_recv[k - 1, 0:1, :], 0.0
                )
            old = jnp.sum(placed.T, axis=0, keepdims=True)
            rest = base_ref[...] - old
            length = jnp.broadcast_to(lengths_ref[...], (1, tok))
            scale = jnp.where(
                lax.broadcasted_iota(jnp.int32, (1, tok), 1) < length,
                -loss_scale * jnp.broadcast_to(advantage_ref[...], (1, tok)) / length.astype(f32),
                0.0,
            )
        for k in range(1, n_resp):
            for x in range(2):
                prefix_copy(k, h, x).wait_recv()
        for g in range(0, GQ, PAIR):
            cols = pl.ds(g * HD, PAIR * HD)
            scores = scores_of(far_kv, far_bias, h, g)
            own_top = stats[h, 0:1, cols]
            top = jnp.maximum(own_top, jnp.max(scores, axis=0, keepdims=True))
            shifted = jnp.exp2(scores - top)
            toward = toward_of(far_kv, h, g)
            shrink = jnp.exp2(own_top - top)
            inverse = 1.0 / (
                shrink * stats[h, 1:2, cols] + jnp.sum(shifted, axis=0, keepdims=True)
            )
            weight = shrink * inverse
            prob = shifted * inverse
            delta = weight * stats[h, 2:3, cols] + jnp.sum(prob * toward, axis=0, keepdims=True)
            far_prob[h, :, cols] = prob.astype(bf16)
            far_core[h, :, cols] = (prob * (toward - delta)).astype(bf16)
            stats[h, 0:1, cols] = delta
            stats[h, 1:2, cols] = weight
            for i in range(PAIR):
                gained = gained + delta[:, i * HD : (i + 1) * HD]

    coeff = scale * jnp.clip(jnp.exp(gained + rest), clip_lower, clip_upper)
    coeff_rows = jnp.broadcast_to(coeff, (tok, tok)).T
    score_rows = coeff_rows * score_scale

    for h in range(KVH):
        for x, source, weights, factor in (
            (0, q_ref, far_core, score_rows),
            (1, d_ref, far_prob, coeff_rows),
        ):
            rows = jnp.concatenate(
                [
                    (source[:, pl.ds(h * width + g * HD, HD)].astype(f32) * factor).astype(bf16)
                    for g in range(GQ)
                ],
                axis=0,
            )
            rows_ref[h, x] = rows
            grad = dot(weights[h], rows, ((1,), (0,))).astype(bf16)
            for k in range(1, n_resp):
                part_send[h, k - 1, x] = grad[(k - 1) * shard : k * shard]
        for k in range(1, n_resp):
            part_copy(k, h).start()

    for h in range(KVH):
        cores, probs = [], []
        for g in range(0, GQ, PAIR):
            cols = pl.ds(g * HD, PAIR * HD)
            toward = toward_of(own_kv, h, g)
            prob = own_prob[h, :, cols].astype(f32) * stats[h, 1:2, cols]
            cores.append((prob * (toward - stats[h, 0:1, cols])).astype(bf16))
            probs.append(prob.astype(bf16))
        core = jnp.concatenate(cores, axis=1)
        for x, weights in ((0, core), (1, jnp.concatenate(probs, axis=1))):
            grad = dot(weights, rows_ref[h, x], ((1,), (0,)))
            own_part[:, kv_cols(h, x)] = grad[:shard]
            rg_ref[:, kv_cols(h, x)] = grad[shard:].astype(bf16)
        grad = dot(own_kv[:, kv_cols(h, 0)], core, ((0,), (0,))) + dot(
            far_kv[:, kv_cols(h, 0)], far_core[h], ((0,), (0,))
        )
        for g in range(GQ):
            one = grad[:, g * HD : (g + 1) * HD] * (coeff * score_scale)
            qg_ref[:, pl.ds(h * width + g * HD, HD)] = one.T.astype(bf16)

    for h in range(KVH):
        for k in range(1, n_resp):
            part_copy(k, h).wait_recv()
        for x in range(2):
            summed = own_part[:, kv_cols(h, x)]
            for k in range(1, n_resp):
                summed = summed + part_recv[h, k - 1, x].astype(f32)
            pg_ref[:, kv_cols(h, x)] = summed.astype(bf16)

    for k in range(1, n_dp):
        row_copy(k).wait_send()
    for h in range(KVH):
        for k in range(1, n_resp):
            for x in range(2):
                prefix_copy(k, h, x).wait_send()
            part_copy(k, h).wait_send()


def deliver(*refs):
    count = len(refs) // 2
    sems = refs[-1]
    copies = [
        pltpu.make_async_copy(refs[i], refs[count + i], sems.at[i]) for i in range(count)
    ]
    for copy in copies:
        copy.start()
    for copy in copies:
        copy.wait()


def body(
    queries,
    prefix_kv,
    resp_kv,
    direction,
    base_logprob,
    rollout_logprob,
    destination,
    advantage,
    lengths,
    prefix_blocks,
):
    n_dp, n_resp = lax.axis_size("dp"), lax.axis_size("resp")
    tok = queries.shape[2]
    shard, kv_width = prefix_kv.shape[1:]
    own_rows = shard + tok
    far_rows = (n_resp - 1) * shard
    columns = QH * HD
    hbm_spec = pl.BlockSpec(memory_space=pltpu.HBM)
    vmem_spec = pl.BlockSpec(memory_space=pltpu.VMEM)
    dma = pltpu.SemaphoreType.DMA
    i32 = jnp.int32
    shapes = ((tok, columns), (tok, kv_width), (shard, kv_width))
    run = pl.pallas_call(
        functools.partial(kernel, n_dp, n_resp),
        out_shape=tuple(pltpu.VMEM(s, bf16) for s in shapes),
        in_specs=[hbm_spec] * 10,
        out_specs=(vmem_spec,) * 3,
        scratch_shapes=[
            pltpu.VMEM((tok, columns), bf16),
            pltpu.VMEM((tok, columns), bf16),
            pltpu.VMEM((own_rows, kv_width), bf16),
            pltpu.VMEM((far_rows, kv_width), bf16),
            pltpu.VMEM((KVH, own_rows, GQ * tok), bf16),
            pltpu.VMEM((KVH, far_rows, GQ * tok), bf16),
            pltpu.VMEM((KVH, far_rows, GQ * tok), bf16),
            pltpu.VMEM((own_rows, tok), f32),
            pltpu.VMEM((far_rows, tok), f32),
            pltpu.VMEM((KVH, 3, GQ * tok), f32),
            pltpu.VMEM((KVH, 2, GQ * tok, HD), bf16),
            pltpu.VMEM((shard, kv_width), f32),
            pltpu.VMEM((8, tok), f32),
            pltpu.VMEM((n_dp - 1, 8, tok), f32),
            pltpu.VMEM((KVH, n_resp - 1, 2, shard, HD), bf16),
            pltpu.VMEM((KVH, n_resp - 1, 2, shard, HD), bf16),
            pltpu.VMEM((1, tok), f32),
            pltpu.VMEM((1, tok), f32),
            pltpu.VMEM((1, tok), i32),
            pltpu.VMEM((1, 1), f32),
            pltpu.VMEM((1, 1), i32),
            pltpu.VMEM((1, 1), i32),
            dma((KVH, 2)),
            dma((2,)),
            dma((6,)),
            dma((n_resp - 1, KVH, 2)),
            dma((n_resp - 1, KVH, 2)),
            dma((n_dp - 1,)),
            dma((n_dp - 1,)),
            dma((n_resp - 1, KVH)),
            dma((n_resp - 1, KVH)),
            pltpu.SemaphoreType.REGULAR,
        ],
        compiler_params=pltpu.CompilerParams(
            collective_id=0, has_side_effects=True, vmem_limit_bytes=56 << 20
        ),
    )
    grads = lax.cond(
        lax.axis_index("dp") >= 0,
        lambda *operands: tuple(run(*operands[:4], *[pltpu.with_memory_space_constraint(o, pltpu.HBM) for o in operands[4:]])),
        lambda *operands: tuple(jnp.zeros(s, bf16) for s in shapes),
        queries[0, 0],
        prefix_kv[0],
        resp_kv[0, 0],
        direction[0, 0],
        base_logprob[0],
        rollout_logprob[0],
        destination[0],
        advantage,
        lengths,
        prefix_blocks,
    )
    query_grad, resp_grad, prefix_grad = pl.pallas_call(
        deliver,
        out_shape=tuple(jax.ShapeDtypeStruct(g.shape, g.dtype) for g in grads),
        in_specs=[vmem_spec] * 3,
        out_specs=(pl.BlockSpec(memory_space=pl.ANY),) * 3,
        scratch_shapes=[dma((3,))],
    )(*[pltpu.with_memory_space_constraint(g, pltpu.VMEM) for g in grads])
    return query_grad[None, None], resp_grad[None, None], prefix_grad[None]


def solution(mesh):
    return jax.shard_map(
        body,
        mesh=mesh,
        in_specs=(
            P("dp", "resp", None, None),
            P("dp", "resp", None),
            P("dp", "resp", None, None),
            P("dp", "resp", None, None),
            P("dp", "resp", None),
            P("dp", "resp", None),
            P("dp", "resp", None),
            P("dp", "resp"),
            P("dp", "resp"),
            P("dp", "resp"),
        ),
        out_specs=(P("dp", "resp", None, None), P("dp", "resp", None, None), P("dp", "resp", None)),
        check_vma=False,
    )
```

```python
import functools
import math

import jax
import jax.numpy as jnp
from jax import lax
from jax.experimental import pallas as pl
from jax.experimental.pallas import tpu as pltpu
from jax.sharding import PartitionSpec as P

QH = 32
KVH = 4
HD = 128
GQ = 8
BLOCK = 128
PAIR = 4

loss_scale = 65536.0
clip_lower = 0.8
clip_upper = 1.28
score_scale = 1.0 / math.sqrt(HD)
exp2_scale = score_scale * math.log2(math.e)
masked = -1e30

MESH = pl.DeviceIdType.MESH
bf16, f32 = jnp.bfloat16, jnp.float32


def dot(a, b, dims):
    return lax.dot_general(a, b, (dims, ((), ())), preferred_element_type=f32)


def kernel(
    n_dp,
    n_resp,
    queries_hbm,
    prefix_hbm,
    resp_hbm,
    direction_hbm,
    base_hbm,
    rollout_hbm,
    destination_hbm,
    advantage_ref,
    lengths_ref,
    blocks_ref,
    qg_ref,
    rg_ref,
    pg_ref,
    q_ref,
    d_ref,
    own_kv,
    far_kv,
    own_prob,
    far_prob,
    far_core,
    own_bias,
    far_bias,
    stats,
    rows_ref,
    own_part,
    row_send,
    row_recv,
    part_send,
    part_recv,
    base_ref,
    rollout_ref,
    destination_ref,
    load_sems,
    own_sem,
    small_sems,
    prefix_send_sem,
    prefix_recv_sems,
    row_send_sem,
    row_recv_sem,
    part_send_sem,
    part_recv_sems,
    ready_sem,
):
    my_dp, my_resp = lax.axis_index("dp"), lax.axis_index("resp")
    tok = q_ref.shape[0]
    shard = prefix_hbm.shape[0]
    own_rows = own_kv.shape[0]
    far_rows = far_kv.shape[0]
    width = GQ * HD

    def head_cols(h):
        return pl.ds(h * width, width)

    def kv_cols(h, x):
        return pl.ds((x * KVH + h) * HD, HD)

    def load_copies(h):
        return (
            pltpu.make_async_copy(
                queries_hbm.at[:, head_cols(h)], q_ref.at[:, head_cols(h)], load_sems.at[h]
            ),
            pltpu.make_async_copy(
                direction_hbm.at[:, head_cols(h)], d_ref.at[:, head_cols(h)], load_sems.at[h]
            ),
        )

    def wait_bytes(ref, sem):
        pltpu.make_async_copy(ref, ref, sem).wait()

    own_copies = (
        pltpu.make_async_copy(prefix_hbm, own_kv.at[pl.ds(0, shard), :], own_sem),
        pltpu.make_async_copy(resp_hbm, own_kv.at[pl.ds(shard, tok), :], own_sem),
    )
    small_copies = [
        pltpu.make_async_copy(source, target, small_sems.at[i])
        for i, (source, target) in enumerate(
            (
                (rollout_hbm, rollout_ref),
                (destination_hbm, destination_ref),
                (base_hbm, base_ref),
            )
        )
    ]

    if n_resp == 4:
        column, line = lax.rem(my_resp, 2), my_resp // 2
        after = before = {
            1: my_resp + 1 - 2 * column,
            2: my_resp + 2 - 4 * line,
            3: 3 - my_resp,
        }
    else:
        after = {k: lax.rem(my_resp + k, n_resp) for k in range(1, n_resp)}
        before = {k: lax.rem(my_resp + n_resp - k, n_resp) for k in range(1, n_resp)}
    order = range(n_resp - 1, 0, -1)

    def resp_peer(k):
        return (my_dp, after[k])

    def dp_peer(k):
        return (lax.rem(my_dp + k, n_dp), my_resp)

    def prefix_copy(k, h, x):
        return pltpu.make_async_remote_copy(
            src_ref=prefix_hbm.at[:, kv_cols(h, x)],
            dst_ref=far_kv.at[pl.ds((k - 1) * shard, shard), kv_cols(h, x)],
            send_sem=prefix_send_sem,
            recv_sem=prefix_recv_sems.at[h],
            device_id=resp_peer(k),
            device_id_type=MESH,
        )

    def row_copy(k):
        return pltpu.make_async_remote_copy(
            src_ref=row_send,
            dst_ref=row_recv.at[k - 1],
            send_sem=row_send_sem,
            recv_sem=row_recv_sem,
            device_id=dp_peer(k),
            device_id_type=MESH,
        )

    def part_copy(k, h):
        return pltpu.make_async_remote_copy(
            src_ref=part_send.at[h, k - 1],
            dst_ref=part_recv.at[h, k - 1],
            send_sem=part_send_sem,
            recv_sem=part_recv_sems.at[h],
            device_id=(my_dp, before[k]),
            device_id_type=MESH,
        )

    barrier = pltpu.get_barrier_semaphore()
    for k in range(1, n_resp):
        pl.semaphore_signal(barrier, inc=1, device_id=resp_peer(k), device_id_type=MESH)
    for k in range(1, n_dp):

        @pl.when(my_dp + k < n_dp)
        def _(k=k):
            pl.semaphore_signal(barrier, inc=1, device_id=dp_peer(k), device_id_type=MESH)

    for copy in own_copies:
        copy.start()
    for h in range(KVH):
        for copy in load_copies(h):
            copy.start()
    for copy in small_copies:
        copy.start()

    pl.semaphore_wait(barrier, n_resp - 1 + my_dp)
    second = lax.rem(my_dp, 2)

    def send_prefix():
        for h in range(KVH):
            for k in order:
                for x in range(2):
                    prefix_copy(k, h, x).start()

    pl.when(second == 1)(send_prefix)
    for copy in small_copies:
        copy.wait()
    row_send[...] = jnp.zeros_like(row_send)
    row_send[0:1, :] = rollout_ref[...]
    row_send[1:2, :] = destination_ref[...].astype(f32)
    for k in range(1, n_dp):

        @pl.when(my_dp + k >= n_dp)
        def _(k=k):
            pl.semaphore_signal(ready_sem, inc=1, device_id=dp_peer(k), device_id_type=MESH)
            row_copy(k).start()

    visible = blocks_ref[0, 0] * BLOCK
    key_index = lax.broadcasted_iota(jnp.int32, (own_rows, tok), 0)
    query_index = lax.broadcasted_iota(jnp.int32, (own_rows, tok), 1)
    allowed = ((key_index < shard) & (key_index + my_resp * shard < visible)) | (
        (key_index >= shard) & (key_index - shard <= query_index)
    )
    own_bias[...] = jnp.where(allowed, 0.0, masked)
    place = lax.broadcasted_iota(jnp.int32, (shard, tok), 0)
    for k in range(1, n_resp):
        row = place + before[k] * shard
        far_bias[pl.ds((k - 1) * shard, shard), :] = jnp.where(row < visible, 0.0, masked)

    def stack(ref, h, g):
        return jnp.concatenate(
            [ref[:, pl.ds(h * width + (g + i) * HD, HD)] for i in range(PAIR)], axis=0
        )

    def scores_of(kv, bias_ref, h, g):
        bias = jnp.concatenate([bias_ref[...]] * PAIR, axis=1)
        return dot(kv[:, kv_cols(h, 0)], stack(q_ref, h, g), ((1,), (1,))) * exp2_scale + bias

    def toward_of(kv, h, g):
        return dot(kv[:, kv_cols(h, 1)], stack(d_ref, h, g), ((1,), (1,)))

    wait_bytes(own_kv, own_sem)

    for h in range(KVH):
        wait_bytes(q_ref.at[:, pl.ds(0, 2 * width)], load_sems.at[h])
        for g in range(0, GQ, PAIR):
            cols = pl.ds(g * HD, PAIR * HD)
            scores = scores_of(own_kv, own_bias, h, g)
            top = jnp.max(scores, axis=0, keepdims=True)
            prob = jnp.exp2(scores - top)
            toward = toward_of(own_kv, h, g)
            stats[h, 0:1, cols] = top
            stats[h, 1:2, cols] = jnp.sum(prob, axis=0, keepdims=True)
            stats[h, 2:3, cols] = jnp.sum(prob * toward, axis=0, keepdims=True)
            own_prob[h, :, cols] = prob.astype(bf16)
        if h == 1:
            pl.when(second == 0)(send_prefix)

    @pl.when(my_dp < n_dp - 1)
    def _():
        pl.semaphore_wait(ready_sem, n_dp - 1 - my_dp)

    for k in range(1, n_dp):

        @pl.when(my_dp + k < n_dp)
        def _(k=k):
            row_copy(k).start()

    gained = jnp.zeros((1, tok), f32)
    for h in range(KVH):
        if h == KVH - 1:
            slot = (lax.broadcasted_iota(jnp.int32, (tok, tok), 0) + my_dp * tok).astype(f32)
            placed = jnp.where(row_send[1:2, :] == slot, row_send[0:1, :], 0.0)
            wait_bytes(row_recv, row_recv_sem)
            for k in range(1, n_dp):
                placed = placed + jnp.where(
                    row_recv[k - 1, 1:2, :] == slot, row_recv[k - 1, 0:1, :], 0.0
                )
            old = jnp.sum(placed.T, axis=0, keepdims=True)
            rest = base_ref[...] - old
            length = lengths_ref[0, 0]
            scale = jnp.where(
                lax.broadcasted_iota(jnp.int32, (1, tok), 1) < length,
                -loss_scale * advantage_ref[0, 0] / length.astype(f32),
                0.0,
            )
        wait_bytes(far_kv.at[:, pl.ds(0, 2 * HD)], prefix_recv_sems.at[h])
        for g in range(0, GQ, PAIR):
            cols = pl.ds(g * HD, PAIR * HD)
            scores = scores_of(far_kv, far_bias, h, g)
            own_top = stats[h, 0:1, cols]
            top = jnp.maximum(own_top, jnp.max(scores, axis=0, keepdims=True))
            shifted = jnp.exp2(scores - top)
            toward = toward_of(far_kv, h, g)
            shrink = jnp.exp2(own_top - top)
            inverse = 1.0 / (
                shrink * stats[h, 1:2, cols] + jnp.sum(shifted, axis=0, keepdims=True)
            )
            weight = shrink * inverse
            prob = shifted * inverse
            delta = weight * stats[h, 2:3, cols] + jnp.sum(prob * toward, axis=0, keepdims=True)
            far_prob[h, :, cols] = prob.astype(bf16)
            far_core[h, :, cols] = (prob * (toward - delta)).astype(bf16)
            stats[h, 0:1, cols] = delta
            stats[h, 1:2, cols] = weight
            for i in range(PAIR):
                gained = gained + delta[:, i * HD : (i + 1) * HD]

    coeff = scale * jnp.clip(jnp.exp(gained + rest), clip_lower, clip_upper)
    coeff_rows = jnp.broadcast_to(coeff, (tok, tok)).T
    score_rows = coeff_rows * score_scale

    for h in range(KVH):
        for x, source, weights, factor in (
            (0, q_ref, far_core, score_rows),
            (1, d_ref, far_prob, coeff_rows),
        ):
            rows = jnp.concatenate(
                [
                    (source[:, pl.ds(h * width + g * HD, HD)].astype(f32) * factor).astype(bf16)
                    for g in range(GQ)
                ],
                axis=0,
            )
            rows_ref[h, x] = rows
            grad = dot(weights[h], rows, ((1,), (0,))).astype(bf16)
            for k in range(1, n_resp):
                part_send[h, k - 1, x] = grad[(k - 1) * shard : k * shard]
        for k in order:
            part_copy(k, h).start()

    for h in range(KVH):
        cores, probs = [], []
        for g in range(0, GQ, PAIR):
            cols = pl.ds(g * HD, PAIR * HD)
            toward = toward_of(own_kv, h, g)
            prob = own_prob[h, :, cols].astype(f32) * stats[h, 1:2, cols]
            cores.append((prob * (toward - stats[h, 0:1, cols])).astype(bf16))
            probs.append(prob.astype(bf16))
        core = jnp.concatenate(cores, axis=1)
        for x, weights in ((0, core), (1, jnp.concatenate(probs, axis=1))):
            grad = dot(weights, rows_ref[h, x], ((1,), (0,)))
            own_part[:, kv_cols(h, x)] = grad[:shard]
            rg_ref[:, kv_cols(h, x)] = grad[shard:].astype(bf16)
        grad = dot(own_kv[:, kv_cols(h, 0)], core, ((0,), (0,))) + dot(
            far_kv[:, kv_cols(h, 0)], far_core[h], ((0,), (0,))
        )
        for g in range(GQ):
            one = grad[:, g * HD : (g + 1) * HD] * (coeff * score_scale)
            qg_ref[:, pl.ds(h * width + g * HD, HD)] = one.T.astype(bf16)

    for h in range(KVH):
        wait_bytes(part_recv.at[h], part_recv_sems.at[h])
        for x in range(2):
            summed = own_part[:, kv_cols(h, x)]
            for k in range(1, n_resp):
                summed = summed + part_recv[h, k - 1, x].astype(f32)
            pg_ref[:, kv_cols(h, x)] = summed.astype(bf16)

    wait_bytes(row_recv, row_send_sem)
    wait_bytes(far_kv, prefix_send_sem)
    wait_bytes(part_send, part_send_sem)


def deliver(*refs):
    count = len(refs) // 2
    sems = refs[-1]
    copies = [
        pltpu.make_async_copy(refs[i], refs[count + i], sems.at[i]) for i in range(count)
    ]
    for copy in copies:
        copy.start()
    for copy in copies:
        copy.wait()


def body(
    queries,
    prefix_kv,
    resp_kv,
    direction,
    base_logprob,
    rollout_logprob,
    destination,
    advantage,
    lengths,
    prefix_blocks,
):
    n_dp, n_resp = lax.axis_size("dp"), lax.axis_size("resp")
    tok = queries.shape[2]
    shard, kv_width = prefix_kv.shape[1:]
    own_rows = shard + tok
    far_rows = (n_resp - 1) * shard
    columns = QH * HD
    vmem_spec = pl.BlockSpec(memory_space=pltpu.VMEM)
    dma = pltpu.SemaphoreType.DMA
    i32 = jnp.int32
    shapes = ((tok, columns), (tok, kv_width), (shard, kv_width))
    grads = pl.pallas_call(
        functools.partial(kernel, n_dp, n_resp),
        out_shape=tuple(pltpu.VMEM(s, bf16) for s in shapes),
        in_specs=[pl.BlockSpec(memory_space=pl.ANY)] * 7 + [pl.BlockSpec(memory_space=pltpu.SMEM)] * 3,
        out_specs=(vmem_spec,) * 3,
        scratch_shapes=[
            pltpu.VMEM((tok, columns), bf16),
            pltpu.VMEM((tok, columns), bf16),
            pltpu.VMEM((own_rows, kv_width), bf16),
            pltpu.VMEM((far_rows, kv_width), bf16),
            pltpu.VMEM((KVH, own_rows, GQ * tok), bf16),
            pltpu.VMEM((KVH, far_rows, GQ * tok), bf16),
            pltpu.VMEM((KVH, far_rows, GQ * tok), bf16),
            pltpu.VMEM((own_rows, tok), f32),
            pltpu.VMEM((far_rows, tok), f32),
            pltpu.VMEM((KVH, 3, GQ * tok), f32),
            pltpu.VMEM((KVH, 2, GQ * tok, HD), bf16),
            pltpu.VMEM((shard, kv_width), f32),
            pltpu.VMEM((8, tok), f32),
            pltpu.VMEM((n_dp - 1, 8, tok), f32),
            pltpu.VMEM((KVH, n_resp - 1, 2, shard, HD), bf16),
            pltpu.VMEM((KVH, n_resp - 1, 2, shard, HD), bf16),
            pltpu.VMEM((1, tok), f32),
            pltpu.VMEM((1, tok), f32),
            pltpu.VMEM((1, tok), i32),
            dma((KVH,)),
            dma,
            dma((3,)),
            dma,
            dma((KVH,)),
            dma,
            dma,
            dma,
            dma((KVH,)),
            pltpu.SemaphoreType.REGULAR,
        ],
        compiler_params=pltpu.CompilerParams(
            collective_id=0, has_side_effects=True, vmem_limit_bytes=56 << 20
        ),
    )(
        queries[0, 0],
        prefix_kv[0],
        resp_kv[0, 0],
        direction[0, 0],
        base_logprob[0],
        rollout_logprob[0],
        destination[0],
        advantage,
        lengths,
        prefix_blocks,
    )
    query_grad, resp_grad, prefix_grad = pl.pallas_call(
        deliver,
        out_shape=tuple(jax.ShapeDtypeStruct(g.shape, g.dtype) for g in grads),
        in_specs=[vmem_spec] * 3,
        out_specs=(pl.BlockSpec(memory_space=pl.ANY),) * 3,
        scratch_shapes=[dma((3,))],
    )(*[pltpu.with_memory_space_constraint(g, pltpu.VMEM) for g in grads])
    return query_grad[None, None], resp_grad[None, None], prefix_grad[None]


def solution(mesh):
    return jax.shard_map(
        body,
        mesh=mesh,
        in_specs=(
            P("dp", "resp", None, None),
            P("dp", "resp", None),
            P("dp", "resp", None, None),
            P("dp", "resp", None, None),
            P("dp", "resp", None),
            P("dp", "resp", None),
            P("dp", "resp", None),
            P("dp", "resp"),
            P("dp", "resp"),
            P("dp", "resp"),
        ),
        out_specs=(P("dp", "resp", None, None), P("dp", "resp", None, None), P("dp", "resp", None)),
        check_vma=False,
    )
```

```python
import functools
import math

import jax
import jax.numpy as jnp
from jax import lax
from jax.experimental import pallas as pl
from jax.experimental.pallas import tpu as pltpu
from jax.sharding import PartitionSpec as P

QH = 32
KVH = 4
HD = 128
GQ = 8
BLOCK = 128
PAIR = 4

loss_scale = 65536.0
clip_lower = 0.8
clip_upper = 1.28
score_scale = 1.0 / math.sqrt(HD)
exp2_scale = score_scale * math.log2(math.e)
masked = -1e30

MESH = pl.DeviceIdType.MESH
bf16, f32 = jnp.bfloat16, jnp.float32


def dot(a, b, dims):
    return lax.dot_general(a, b, (dims, ((), ())), preferred_element_type=f32)


def kernel(
    n_dp,
    n_resp,
    queries_hbm,
    prefix_hbm,
    resp_hbm,
    direction_hbm,
    base_hbm,
    rollout_hbm,
    destination_hbm,
    advantage_ref,
    lengths_ref,
    blocks_ref,
    qg_ref,
    rg_ref,
    pg_ref,
    q_ref,
    d_ref,
    own_kv,
    far_kv,
    own_prob,
    far_prob,
    far_core,
    own_bias,
    far_bias,
    stats,
    rows_ref,
    own_part,
    row_send,
    row_recv,
    part_send,
    part_recv,
    base_ref,
    rollout_ref,
    destination_ref,
    load_sems,
    own_sem,
    small_sems,
    prefix_send_sem,
    prefix_recv_sems,
    row_send_sem,
    row_recv_sem,
    part_send_sem,
    part_recv_sems,
    ready_sem,
):
    my_dp, my_resp = lax.axis_index("dp"), lax.axis_index("resp")
    tok = q_ref.shape[0]
    shard = prefix_hbm.shape[0]
    own_rows = own_kv.shape[0]
    far_rows = far_kv.shape[0]
    width = GQ * HD

    def head_cols(h):
        return pl.ds(h * width, width)

    def kv_cols(h, x):
        return pl.ds((x * KVH + h) * HD, HD)

    def load_copies(h):
        return (
            pltpu.make_async_copy(
                queries_hbm.at[:, head_cols(h)], q_ref.at[:, head_cols(h)], load_sems.at[h]
            ),
            pltpu.make_async_copy(
                direction_hbm.at[:, head_cols(h)], d_ref.at[:, head_cols(h)], load_sems.at[h]
            ),
        )

    def wait_bytes(ref, sem):
        pltpu.make_async_copy(ref, ref, sem).wait()

    own_copies = (
        pltpu.make_async_copy(prefix_hbm, own_kv.at[pl.ds(0, shard), :], own_sem),
        pltpu.make_async_copy(resp_hbm, own_kv.at[pl.ds(shard, tok), :], own_sem),
    )
    small_copies = [
        pltpu.make_async_copy(source, target, small_sems.at[i])
        for i, (source, target) in enumerate(
            (
                (rollout_hbm, rollout_ref),
                (destination_hbm, destination_ref),
                (base_hbm, base_ref),
            )
        )
    ]

    if n_resp == 4:
        column, line = lax.rem(my_resp, 2), my_resp // 2
        after = before = {
            1: my_resp + 1 - 2 * column,
            2: my_resp + 2 - 4 * line,
            3: 3 - my_resp,
        }
    else:
        after = {k: lax.rem(my_resp + k, n_resp) for k in range(1, n_resp)}
        before = {k: lax.rem(my_resp + n_resp - k, n_resp) for k in range(1, n_resp)}
    order = range(n_resp - 1, 0, -1)

    def resp_peer(k):
        return (my_dp, after[k])

    def dp_peer(k):
        return (lax.rem(my_dp + k, n_dp), my_resp)

    def prefix_copy(k, h, x):
        return pltpu.make_async_remote_copy(
            src_ref=prefix_hbm.at[:, kv_cols(h, x)],
            dst_ref=far_kv.at[pl.ds((k - 1) * shard, shard), kv_cols(h, x)],
            send_sem=prefix_send_sem,
            recv_sem=prefix_recv_sems.at[h],
            device_id=resp_peer(k),
            device_id_type=MESH,
        )

    def row_copy(k):
        return pltpu.make_async_remote_copy(
            src_ref=row_send,
            dst_ref=row_recv.at[k - 1],
            send_sem=row_send_sem,
            recv_sem=row_recv_sem,
            device_id=dp_peer(k),
            device_id_type=MESH,
        )

    def part_copy(k, h):
        return pltpu.make_async_remote_copy(
            src_ref=part_send.at[h, k - 1],
            dst_ref=part_recv.at[h, k - 1],
            send_sem=part_send_sem,
            recv_sem=part_recv_sems.at[h],
            device_id=(my_dp, before[k]),
            device_id_type=MESH,
        )

    barrier = pltpu.get_barrier_semaphore()
    for k in range(1, n_resp):
        pl.semaphore_signal(barrier, inc=1, device_id=resp_peer(k), device_id_type=MESH)
    for k in range(1, n_dp):

        @pl.when(my_dp + k < n_dp)
        def _(k=k):
            pl.semaphore_signal(barrier, inc=1, device_id=dp_peer(k), device_id_type=MESH)

    for copy in own_copies:
        copy.start()
    for h in range(KVH):
        for copy in load_copies(h):
            copy.start()
    for copy in small_copies:
        copy.start()

    pl.semaphore_wait(barrier, n_resp - 1 + my_dp)
    second = lax.rem(my_dp, 2)

    def send_prefix():
        for h in range(KVH):
            for x in range(2):
                for k in order:
                    prefix_copy(k, h, x).start()

    pl.when(second == 1)(send_prefix)
    for copy in small_copies:
        copy.wait()
    row_send[...] = jnp.zeros_like(row_send)
    row_send[0:1, :] = rollout_ref[...]
    row_send[1:2, :] = destination_ref[...].astype(f32)
    for k in range(1, n_dp):

        @pl.when(my_dp + k >= n_dp)
        def _(k=k):
            pl.semaphore_signal(ready_sem, inc=1, device_id=dp_peer(k), device_id_type=MESH)
            row_copy(k).start()

    visible = blocks_ref[0, 0] * BLOCK
    key_index = lax.broadcasted_iota(jnp.int32, (own_rows, tok), 0)
    query_index = lax.broadcasted_iota(jnp.int32, (own_rows, tok), 1)
    allowed = ((key_index < shard) & (key_index + my_resp * shard < visible)) | (
        (key_index >= shard) & (key_index - shard <= query_index)
    )
    own_bias[...] = jnp.where(allowed, 0.0, masked)
    place = lax.broadcasted_iota(jnp.int32, (shard, tok), 0)
    for k in range(1, n_resp):
        row = place + before[k] * shard
        far_bias[pl.ds((k - 1) * shard, shard), :] = jnp.where(row < visible, 0.0, masked)

    def stack(ref, h, g):
        return jnp.concatenate(
            [ref[:, pl.ds(h * width + (g + i) * HD, HD)] for i in range(PAIR)], axis=0
        )

    def scores_of(kv, bias_ref, h, g):
        bias = jnp.concatenate([bias_ref[...]] * PAIR, axis=1)
        return dot(kv[:, kv_cols(h, 0)], stack(q_ref, h, g), ((1,), (1,))) * exp2_scale + bias

    def toward_of(kv, h, g):
        return dot(kv[:, kv_cols(h, 1)], stack(d_ref, h, g), ((1,), (1,)))

    wait_bytes(own_kv, own_sem)

    for h in range(KVH):
        wait_bytes(q_ref.at[:, pl.ds(0, 2 * width)], load_sems.at[h])
        for g in range(0, GQ, PAIR):
            cols = pl.ds(g * HD, PAIR * HD)
            scores = scores_of(own_kv, own_bias, h, g)
            top = jnp.max(scores, axis=0, keepdims=True)
            prob = jnp.exp2(scores - top)
            toward = toward_of(own_kv, h, g)
            stats[h, 0:1, cols] = top
            stats[h, 1:2, cols] = jnp.sum(prob, axis=0, keepdims=True)
            stats[h, 2:3, cols] = jnp.sum(prob * toward, axis=0, keepdims=True)
            own_prob[h, :, cols] = prob.astype(bf16)
        if h == 1:
            pl.when(second == 0)(send_prefix)

    @pl.when(my_dp < n_dp - 1)
    def _():
        pl.semaphore_wait(ready_sem, n_dp - 1 - my_dp)

    for k in range(1, n_dp):

        @pl.when(my_dp + k < n_dp)
        def _(k=k):
            row_copy(k).start()

    gained = jnp.zeros((1, tok), f32)
    for h in range(KVH):
        if h == KVH - 1:
            slot = (lax.broadcasted_iota(jnp.int32, (tok, tok), 0) + my_dp * tok).astype(f32)
            placed = jnp.where(row_send[1:2, :] == slot, row_send[0:1, :], 0.0)
            wait_bytes(row_recv, row_recv_sem)
            for k in range(1, n_dp):
                placed = placed + jnp.where(
                    row_recv[k - 1, 1:2, :] == slot, row_recv[k - 1, 0:1, :], 0.0
                )
            old = jnp.sum(placed.T, axis=0, keepdims=True)
            rest = base_ref[...] - old
            length = lengths_ref[0, 0]
            scale = jnp.where(
                lax.broadcasted_iota(jnp.int32, (1, tok), 1) < length,
                -loss_scale * advantage_ref[0, 0] / length.astype(f32),
                0.0,
            )
        wait_bytes(far_kv.at[:, pl.ds(0, 2 * HD)], prefix_recv_sems.at[h])
        for g in range(0, GQ, PAIR):
            cols = pl.ds(g * HD, PAIR * HD)
            scores = scores_of(far_kv, far_bias, h, g)
            own_top = stats[h, 0:1, cols]
            top = jnp.maximum(own_top, jnp.max(scores, axis=0, keepdims=True))
            shifted = jnp.exp2(scores - top)
            toward = toward_of(far_kv, h, g)
            shrink = jnp.exp2(own_top - top)
            inverse = 1.0 / (
                shrink * stats[h, 1:2, cols] + jnp.sum(shifted, axis=0, keepdims=True)
            )
            weight = shrink * inverse
            prob = shifted * inverse
            delta = weight * stats[h, 2:3, cols] + jnp.sum(prob * toward, axis=0, keepdims=True)
            far_prob[h, :, cols] = prob.astype(bf16)
            far_core[h, :, cols] = (prob * (toward - delta)).astype(bf16)
            stats[h, 0:1, cols] = delta
            stats[h, 1:2, cols] = weight
            for i in range(PAIR):
                gained = gained + delta[:, i * HD : (i + 1) * HD]

    coeff = scale * jnp.clip(jnp.exp(gained + rest), clip_lower, clip_upper)
    coeff_rows = jnp.broadcast_to(coeff, (tok, tok)).T
    score_rows = coeff_rows * score_scale

    for h in range(KVH):
        for x, source, weights, factor in (
            (0, q_ref, far_core, score_rows),
            (1, d_ref, far_prob, coeff_rows),
        ):
            rows = jnp.concatenate(
                [
                    (source[:, pl.ds(h * width + g * HD, HD)].astype(f32) * factor).astype(bf16)
                    for g in range(GQ)
                ],
                axis=0,
            )
            rows_ref[h, x] = rows
            grad = dot(weights[h], rows, ((1,), (0,))).astype(bf16)
            for k in range(1, n_resp):
                part_send[h, k - 1, x] = grad[(k - 1) * shard : k * shard]
        for k in order:
            part_copy(k, h).start()

    for h in range(KVH):
        cores, probs = [], []
        for g in range(0, GQ, PAIR):
            cols = pl.ds(g * HD, PAIR * HD)
            toward = toward_of(own_kv, h, g)
            prob = own_prob[h, :, cols].astype(f32) * stats[h, 1:2, cols]
            cores.append((prob * (toward - stats[h, 0:1, cols])).astype(bf16))
            probs.append(prob.astype(bf16))
        core = jnp.concatenate(cores, axis=1)
        for x, weights in ((0, core), (1, jnp.concatenate(probs, axis=1))):
            grad = dot(weights, rows_ref[h, x], ((1,), (0,)))
            own_part[:, kv_cols(h, x)] = grad[:shard]
            rg_ref[:, kv_cols(h, x)] = grad[shard:].astype(bf16)
        grad = dot(own_kv[:, kv_cols(h, 0)], core, ((0,), (0,))) + dot(
            far_kv[:, kv_cols(h, 0)], far_core[h], ((0,), (0,))
        )
        for g in range(GQ):
            one = grad[:, g * HD : (g + 1) * HD] * (coeff * score_scale)
            qg_ref[:, pl.ds(h * width + g * HD, HD)] = one.T.astype(bf16)

    for h in range(KVH):
        wait_bytes(part_recv.at[h], part_recv_sems.at[h])
        for x in range(2):
            summed = own_part[:, kv_cols(h, x)]
            for k in range(1, n_resp):
                summed = summed + part_recv[h, k - 1, x].astype(f32)
            pg_ref[:, kv_cols(h, x)] = summed.astype(bf16)

    wait_bytes(row_recv, row_send_sem)
    wait_bytes(far_kv, prefix_send_sem)
    wait_bytes(part_send, part_send_sem)


def deliver(*refs):
    count = len(refs) // 2
    sems = refs[-1]
    copies = [
        pltpu.make_async_copy(refs[i], refs[count + i], sems.at[i]) for i in range(count)
    ]
    for copy in copies:
        copy.start()
    for copy in copies:
        copy.wait()


def body(
    queries,
    prefix_kv,
    resp_kv,
    direction,
    base_logprob,
    rollout_logprob,
    destination,
    advantage,
    lengths,
    prefix_blocks,
):
    n_dp, n_resp = lax.axis_size("dp"), lax.axis_size("resp")
    tok = queries.shape[2]
    shard, kv_width = prefix_kv.shape[1:]
    own_rows = shard + tok
    far_rows = (n_resp - 1) * shard
    columns = QH * HD
    vmem_spec = pl.BlockSpec(memory_space=pltpu.VMEM)
    dma = pltpu.SemaphoreType.DMA
    i32 = jnp.int32
    shapes = ((tok, columns), (tok, kv_width), (shard, kv_width))
    grads = pl.pallas_call(
        functools.partial(kernel, n_dp, n_resp),
        out_shape=tuple(pltpu.VMEM(s, bf16) for s in shapes),
        in_specs=[pl.BlockSpec(memory_space=pl.ANY)] * 7 + [pl.BlockSpec(memory_space=pltpu.SMEM)] * 3,
        out_specs=(vmem_spec,) * 3,
        scratch_shapes=[
            pltpu.VMEM((tok, columns), bf16),
            pltpu.VMEM((tok, columns), bf16),
            pltpu.VMEM((own_rows, kv_width), bf16),
            pltpu.VMEM((far_rows, kv_width), bf16),
            pltpu.VMEM((KVH, own_rows, GQ * tok), bf16),
            pltpu.VMEM((KVH, far_rows, GQ * tok), bf16),
            pltpu.VMEM((KVH, far_rows, GQ * tok), bf16),
            pltpu.VMEM((own_rows, tok), f32),
            pltpu.VMEM((far_rows, tok), f32),
            pltpu.VMEM((KVH, 3, GQ * tok), f32),
            pltpu.VMEM((KVH, 2, GQ * tok, HD), bf16),
            pltpu.VMEM((shard, kv_width), f32),
            pltpu.VMEM((8, tok), f32),
            pltpu.VMEM((n_dp - 1, 8, tok), f32),
            pltpu.VMEM((KVH, n_resp - 1, 2, shard, HD), bf16),
            pltpu.VMEM((KVH, n_resp - 1, 2, shard, HD), bf16),
            pltpu.VMEM((1, tok), f32),
            pltpu.VMEM((1, tok), f32),
            pltpu.VMEM((1, tok), i32),
            dma((KVH,)),
            dma,
            dma((3,)),
            dma,
            dma((KVH,)),
            dma,
            dma,
            dma,
            dma((KVH,)),
            pltpu.SemaphoreType.REGULAR,
        ],
        compiler_params=pltpu.CompilerParams(
            collective_id=0, has_side_effects=True, vmem_limit_bytes=56 << 20
        ),
    )(
        queries[0, 0],
        prefix_kv[0],
        resp_kv[0, 0],
        direction[0, 0],
        base_logprob[0],
        rollout_logprob[0],
        destination[0],
        advantage,
        lengths,
        prefix_blocks,
    )
    query_grad, resp_grad, prefix_grad = pl.pallas_call(
        deliver,
        out_shape=tuple(jax.ShapeDtypeStruct(g.shape, g.dtype) for g in grads),
        in_specs=[vmem_spec] * 3,
        out_specs=(pl.BlockSpec(memory_space=pl.ANY),) * 3,
        scratch_shapes=[dma((3,))],
    )(*[pltpu.with_memory_space_constraint(g, pltpu.VMEM) for g in grads])
    return query_grad[None, None], resp_grad[None, None], prefix_grad[None]


def solution(mesh):
    return jax.shard_map(
        body,
        mesh=mesh,
        in_specs=(
            P("dp", "resp", None, None),
            P("dp", "resp", None),
            P("dp", "resp", None, None),
            P("dp", "resp", None, None),
            P("dp", "resp", None),
            P("dp", "resp", None),
            P("dp", "resp", None),
            P("dp", "resp"),
            P("dp", "resp"),
            P("dp", "resp"),
        ),
        out_specs=(P("dp", "resp", None, None), P("dp", "resp", None, None), P("dp", "resp", None)),
        check_vma=False,
    )
```

```python
import functools
import math

import jax
import jax.numpy as jnp
from jax import lax
from jax.experimental import pallas as pl
from jax.experimental.pallas import tpu as pltpu
from jax.sharding import PartitionSpec as P

QH = 32
KVH = 4
HD = 128
GQ = 8
BLOCK = 128
PAIR = 4

loss_scale = 65536.0
clip_lower = 0.8
clip_upper = 1.28
score_scale = 1.0 / math.sqrt(HD)
exp2_scale = score_scale * math.log2(math.e)
masked = -1e30

MESH = pl.DeviceIdType.MESH
bf16, f32 = jnp.bfloat16, jnp.float32


def dot(a, b, dims):
    return lax.dot_general(a, b, (dims, ((), ())), preferred_element_type=f32)


def kernel(
    n_dp,
    n_resp,
    queries_hbm,
    prefix_hbm,
    resp_hbm,
    direction_hbm,
    base_hbm,
    rollout_hbm,
    destination_hbm,
    advantage_ref,
    lengths_ref,
    blocks_ref,
    qg_ref,
    rg_ref,
    pg_ref,
    q_ref,
    d_ref,
    own_kv,
    far_kv,
    own_prob,
    far_prob,
    far_core,
    own_bias,
    far_bias,
    stats,
    rows_ref,
    own_part,
    row_send,
    row_recv,
    part_send,
    part_recv,
    base_ref,
    rollout_ref,
    destination_ref,
    load_sems,
    own_sem,
    small_sems,
    prefix_send_sem,
    prefix_recv_sems,
    row_send_sem,
    row_recv_sem,
    part_send_sem,
    part_recv_sems,
    ready_sem,
):
    my_dp, my_resp = lax.axis_index("dp"), lax.axis_index("resp")
    tok = q_ref.shape[0]
    shard = prefix_hbm.shape[0]
    own_rows = own_kv.shape[0]
    far_rows = far_kv.shape[0]
    width = GQ * HD

    def head_cols(h):
        return pl.ds(h * width, width)

    def kv_cols(h, x):
        return pl.ds((x * KVH + h) * HD, HD)

    def load_copies(h):
        return (
            pltpu.make_async_copy(
                queries_hbm.at[:, head_cols(h)], q_ref.at[:, head_cols(h)], load_sems.at[h]
            ),
            pltpu.make_async_copy(
                direction_hbm.at[:, head_cols(h)], d_ref.at[:, head_cols(h)], load_sems.at[h]
            ),
        )

    def wait_bytes(ref, sem):
        pltpu.make_async_copy(ref, ref, sem).wait()

    own_copies = (
        pltpu.make_async_copy(prefix_hbm, own_kv.at[pl.ds(0, shard), :], own_sem),
        pltpu.make_async_copy(resp_hbm, own_kv.at[pl.ds(shard, tok), :], own_sem),
    )
    small_copies = [
        pltpu.make_async_copy(source, target, small_sems.at[i])
        for i, (source, target) in enumerate(
            (
                (rollout_hbm, rollout_ref),
                (destination_hbm, destination_ref),
                (base_hbm, base_ref),
            )
        )
    ]

    if n_resp == 4:
        column, line = lax.rem(my_resp, 2), my_resp // 2
        after = before = {
            1: my_resp + 1 - 2 * column,
            2: my_resp + 2 - 4 * line,
            3: 3 - my_resp,
        }
    else:
        after = {k: lax.rem(my_resp + k, n_resp) for k in range(1, n_resp)}
        before = {k: lax.rem(my_resp + n_resp - k, n_resp) for k in range(1, n_resp)}
    order = range(n_resp - 1, 0, -1)

    def resp_peer(k):
        return (my_dp, after[k])

    def dp_peer(k):
        return (lax.rem(my_dp + k, n_dp), my_resp)

    def prefix_copy(k, h, x):
        return pltpu.make_async_remote_copy(
            src_ref=prefix_hbm.at[:, kv_cols(h, x)],
            dst_ref=far_kv.at[pl.ds((k - 1) * shard, shard), kv_cols(h, x)],
            send_sem=prefix_send_sem,
            recv_sem=prefix_recv_sems.at[h],
            device_id=resp_peer(k),
            device_id_type=MESH,
        )

    def row_copy(k):
        return pltpu.make_async_remote_copy(
            src_ref=row_send,
            dst_ref=row_recv.at[k - 1],
            send_sem=row_send_sem,
            recv_sem=row_recv_sem,
            device_id=dp_peer(k),
            device_id_type=MESH,
        )

    def part_copy(k, h):
        return pltpu.make_async_remote_copy(
            src_ref=part_send.at[h, k - 1],
            dst_ref=part_recv.at[h, k - 1],
            send_sem=part_send_sem,
            recv_sem=part_recv_sems.at[h],
            device_id=(my_dp, before[k]),
            device_id_type=MESH,
        )

    barrier = pltpu.get_barrier_semaphore()
    for k in range(1, n_resp):
        pl.semaphore_signal(barrier, inc=1, device_id=resp_peer(k), device_id_type=MESH)
    for k in range(1, n_dp):

        @pl.when(my_dp + k < n_dp)
        def _(k=k):
            pl.semaphore_signal(barrier, inc=1, device_id=dp_peer(k), device_id_type=MESH)

    for copy in own_copies:
        copy.start()
    for h in range(KVH):
        for copy in load_copies(h):
            copy.start()
    for copy in small_copies:
        copy.start()

    pl.semaphore_wait(barrier, n_resp - 1 + my_dp)
    second = lax.rem(my_dp, 2)

    def send_prefix(order=order):
        for h in range(KVH):
            for x in range(2):
                for k in order:
                    prefix_copy(k, h, x).start()

    pl.when(second == 1)(send_prefix)
    for copy in small_copies:
        copy.wait()
    row_send[...] = jnp.zeros_like(row_send)
    row_send[0:1, :] = rollout_ref[...]
    row_send[1:2, :] = destination_ref[...].astype(f32)
    for k in range(1, n_dp):

        @pl.when(my_dp + k >= n_dp)
        def _(k=k):
            pl.semaphore_signal(ready_sem, inc=1, device_id=dp_peer(k), device_id_type=MESH)
            row_copy(k).start()

    visible = blocks_ref[0, 0] * BLOCK
    key_index = lax.broadcasted_iota(jnp.int32, (own_rows, tok), 0)
    query_index = lax.broadcasted_iota(jnp.int32, (own_rows, tok), 1)
    allowed = ((key_index < shard) & (key_index + my_resp * shard < visible)) | (
        (key_index >= shard) & (key_index - shard <= query_index)
    )
    own_bias[...] = jnp.where(allowed, 0.0, masked)
    place = lax.broadcasted_iota(jnp.int32, (shard, tok), 0)
    for k in range(1, n_resp):
        row = place + before[k] * shard
        far_bias[pl.ds((k - 1) * shard, shard), :] = jnp.where(row < visible, 0.0, masked)

    def stack(ref, h, g):
        return jnp.concatenate(
            [ref[:, pl.ds(h * width + (g + i) * HD, HD)] for i in range(PAIR)], axis=0
        )

    def scores_of(kv, bias_ref, h, g):
        bias = jnp.concatenate([bias_ref[...]] * PAIR, axis=1)
        return dot(kv[:, kv_cols(h, 0)], stack(q_ref, h, g), ((1,), (1,))) * exp2_scale + bias

    def toward_of(kv, h, g):
        return dot(kv[:, kv_cols(h, 1)], stack(d_ref, h, g), ((1,), (1,)))

    wait_bytes(own_kv, own_sem)

    for h in range(KVH):
        wait_bytes(q_ref.at[:, pl.ds(0, 2 * width)], load_sems.at[h])
        for g in range(0, GQ, PAIR):
            cols = pl.ds(g * HD, PAIR * HD)
            scores = scores_of(own_kv, own_bias, h, g)
            top = jnp.max(scores, axis=0, keepdims=True)
            prob = jnp.exp2(scores - top)
            toward = toward_of(own_kv, h, g)
            stats[h, 0:1, cols] = top
            stats[h, 1:2, cols] = jnp.sum(prob, axis=0, keepdims=True)
            stats[h, 2:3, cols] = jnp.sum(prob * toward, axis=0, keepdims=True)
            own_prob[h, :, cols] = prob.astype(bf16)
        if h == 1:
            pl.when(second == 0)(functools.partial(send_prefix, order[::-1]))

    @pl.when(my_dp < n_dp - 1)
    def _():
        pl.semaphore_wait(ready_sem, n_dp - 1 - my_dp)

    for k in range(1, n_dp):

        @pl.when(my_dp + k < n_dp)
        def _(k=k):
            row_copy(k).start()

    gained = jnp.zeros((1, tok), f32)
    for h in range(KVH):
        if h == KVH - 1:
            slot = (lax.broadcasted_iota(jnp.int32, (tok, tok), 0) + my_dp * tok).astype(f32)
            placed = jnp.where(row_send[1:2, :] == slot, row_send[0:1, :], 0.0)
            wait_bytes(row_recv, row_recv_sem)
            for k in range(1, n_dp):
                placed = placed + jnp.where(
                    row_recv[k - 1, 1:2, :] == slot, row_recv[k - 1, 0:1, :], 0.0
                )
            old = jnp.sum(placed.T, axis=0, keepdims=True)
            rest = base_ref[...] - old
            length = lengths_ref[0, 0]
            scale = jnp.where(
                lax.broadcasted_iota(jnp.int32, (1, tok), 1) < length,
                -loss_scale * advantage_ref[0, 0] / length.astype(f32),
                0.0,
            )
        wait_bytes(far_kv.at[:, pl.ds(0, 2 * HD)], prefix_recv_sems.at[h])
        for g in range(0, GQ, PAIR):
            cols = pl.ds(g * HD, PAIR * HD)
            scores = scores_of(far_kv, far_bias, h, g)
            own_top = stats[h, 0:1, cols]
            top = jnp.maximum(own_top, jnp.max(scores, axis=0, keepdims=True))
            shifted = jnp.exp2(scores - top)
            toward = toward_of(far_kv, h, g)
            shrink = jnp.exp2(own_top - top)
            inverse = 1.0 / (
                shrink * stats[h, 1:2, cols] + jnp.sum(shifted, axis=0, keepdims=True)
            )
            weight = shrink * inverse
            prob = shifted * inverse
            delta = weight * stats[h, 2:3, cols] + jnp.sum(prob * toward, axis=0, keepdims=True)
            far_prob[h, :, cols] = prob.astype(bf16)
            far_core[h, :, cols] = (prob * (toward - delta)).astype(bf16)
            stats[h, 0:1, cols] = delta
            stats[h, 1:2, cols] = weight
            for i in range(PAIR):
                gained = gained + delta[:, i * HD : (i + 1) * HD]

    coeff = scale * jnp.clip(jnp.exp(gained + rest), clip_lower, clip_upper)
    coeff_rows = jnp.broadcast_to(coeff, (tok, tok)).T
    score_rows = coeff_rows * score_scale

    for h in range(KVH):
        for x, source, weights, factor in (
            (0, q_ref, far_core, score_rows),
            (1, d_ref, far_prob, coeff_rows),
        ):
            rows = jnp.concatenate(
                [
                    (source[:, pl.ds(h * width + g * HD, HD)].astype(f32) * factor).astype(bf16)
                    for g in range(GQ)
                ],
                axis=0,
            )
            rows_ref[h, x] = rows
            grad = dot(weights[h], rows, ((1,), (0,))).astype(bf16)
            for k in range(1, n_resp):
                part_send[h, k - 1, x] = grad[(k - 1) * shard : k * shard]
        for k in order:
            part_copy(k, h).start()

    for h in range(KVH):
        cores, probs = [], []
        for g in range(0, GQ, PAIR):
            cols = pl.ds(g * HD, PAIR * HD)
            toward = toward_of(own_kv, h, g)
            prob = own_prob[h, :, cols].astype(f32) * stats[h, 1:2, cols]
            cores.append((prob * (toward - stats[h, 0:1, cols])).astype(bf16))
            probs.append(prob.astype(bf16))
        core = jnp.concatenate(cores, axis=1)
        for x, weights in ((0, core), (1, jnp.concatenate(probs, axis=1))):
            grad = dot(weights, rows_ref[h, x], ((1,), (0,)))
            own_part[:, kv_cols(h, x)] = grad[:shard]
            rg_ref[:, kv_cols(h, x)] = grad[shard:].astype(bf16)
        grad = dot(own_kv[:, kv_cols(h, 0)], core, ((0,), (0,))) + dot(
            far_kv[:, kv_cols(h, 0)], far_core[h], ((0,), (0,))
        )
        for g in range(GQ):
            one = grad[:, g * HD : (g + 1) * HD] * (coeff * score_scale)
            qg_ref[:, pl.ds(h * width + g * HD, HD)] = one.T.astype(bf16)

    for h in range(KVH):
        wait_bytes(part_recv.at[h], part_recv_sems.at[h])
        for x in range(2):
            summed = own_part[:, kv_cols(h, x)]
            for k in range(1, n_resp):
                summed = summed + part_recv[h, k - 1, x].astype(f32)
            pg_ref[:, kv_cols(h, x)] = summed.astype(bf16)

    wait_bytes(row_recv, row_send_sem)
    wait_bytes(far_kv, prefix_send_sem)
    wait_bytes(part_send, part_send_sem)


def deliver(*refs):
    count = len(refs) // 2
    sems = refs[-1]
    copies = [
        pltpu.make_async_copy(refs[i], refs[count + i], sems.at[i]) for i in range(count)
    ]
    for copy in copies:
        copy.start()
    for copy in copies:
        copy.wait()


def body(
    queries,
    prefix_kv,
    resp_kv,
    direction,
    base_logprob,
    rollout_logprob,
    destination,
    advantage,
    lengths,
    prefix_blocks,
):
    n_dp, n_resp = lax.axis_size("dp"), lax.axis_size("resp")
    tok = queries.shape[2]
    shard, kv_width = prefix_kv.shape[1:]
    own_rows = shard + tok
    far_rows = (n_resp - 1) * shard
    columns = QH * HD
    vmem_spec = pl.BlockSpec(memory_space=pltpu.VMEM)
    dma = pltpu.SemaphoreType.DMA
    i32 = jnp.int32
    shapes = ((tok, columns), (tok, kv_width), (shard, kv_width))
    grads = pl.pallas_call(
        functools.partial(kernel, n_dp, n_resp),
        out_shape=tuple(pltpu.VMEM(s, bf16) for s in shapes),
        in_specs=[pl.BlockSpec(memory_space=pl.ANY)] * 7 + [pl.BlockSpec(memory_space=pltpu.SMEM)] * 3,
        out_specs=(vmem_spec,) * 3,
        scratch_shapes=[
            pltpu.VMEM((tok, columns), bf16),
            pltpu.VMEM((tok, columns), bf16),
            pltpu.VMEM((own_rows, kv_width), bf16),
            pltpu.VMEM((far_rows, kv_width), bf16),
            pltpu.VMEM((KVH, own_rows, GQ * tok), bf16),
            pltpu.VMEM((KVH, far_rows, GQ * tok), bf16),
            pltpu.VMEM((KVH, far_rows, GQ * tok), bf16),
            pltpu.VMEM((own_rows, tok), f32),
            pltpu.VMEM((far_rows, tok), f32),
            pltpu.VMEM((KVH, 3, GQ * tok), f32),
            pltpu.VMEM((KVH, 2, GQ * tok, HD), bf16),
            pltpu.VMEM((shard, kv_width), f32),
            pltpu.VMEM((8, tok), f32),
            pltpu.VMEM((n_dp - 1, 8, tok), f32),
            pltpu.VMEM((KVH, n_resp - 1, 2, shard, HD), bf16),
            pltpu.VMEM((KVH, n_resp - 1, 2, shard, HD), bf16),
            pltpu.VMEM((1, tok), f32),
            pltpu.VMEM((1, tok), f32),
            pltpu.VMEM((1, tok), i32),
            dma((KVH,)),
            dma,
            dma((3,)),
            dma,
            dma((KVH,)),
            dma,
            dma,
            dma,
            dma((KVH,)),
            pltpu.SemaphoreType.REGULAR,
        ],
        compiler_params=pltpu.CompilerParams(
            collective_id=0, has_side_effects=True, vmem_limit_bytes=56 << 20
        ),
    )(
        queries[0, 0],
        prefix_kv[0],
        resp_kv[0, 0],
        direction[0, 0],
        base_logprob[0],
        rollout_logprob[0],
        destination[0],
        advantage,
        lengths,
        prefix_blocks,
    )
    query_grad, resp_grad, prefix_grad = pl.pallas_call(
        deliver,
        out_shape=tuple(jax.ShapeDtypeStruct(g.shape, g.dtype) for g in grads),
        in_specs=[vmem_spec] * 3,
        out_specs=(pl.BlockSpec(memory_space=pl.ANY),) * 3,
        scratch_shapes=[dma((3,))],
    )(*[pltpu.with_memory_space_constraint(g, pltpu.VMEM) for g in grads])
    return query_grad[None, None], resp_grad[None, None], prefix_grad[None]


def solution(mesh):
    return jax.shard_map(
        body,
        mesh=mesh,
        in_specs=(
            P("dp", "resp", None, None),
            P("dp", "resp", None),
            P("dp", "resp", None, None),
            P("dp", "resp", None, None),
            P("dp", "resp", None),
            P("dp", "resp", None),
            P("dp", "resp", None),
            P("dp", "resp"),
            P("dp", "resp"),
            P("dp", "resp"),
        ),
        out_specs=(P("dp", "resp", None, None), P("dp", "resp", None, None), P("dp", "resp", None)),
        check_vma=False,
    )
```
